128 devices in a mesh: heads: 4 (over y_lo, core), seq: 32 (over z, y_hi, x).
Axes of the slice: x: 4, y: 4 (y_hi: 2, y_lo: 2; y = y_hi * 2 + y_lo), z: 4, core: 2. Of those that a mesh axis runs over, the one named last changes fastest.
Arguments:
- queries: bfloat16 [16384, 4096], P('seq', 'heads'), may hold values from -6 to 6
- keys: bfloat16 [16384, 1024], P('seq', 'heads'), may hold values from -6 to 6
- values: bfloat16 [16384, 1024], P('seq', 'heads'), may hold values from -6 to 6
- out: bfloat16 [16384, 4096], P('seq', 'heads'), may hold values from -1.796875 to 1.796875
- output_gradient: bfloat16 [16384, 4096], P('seq', 'heads'), may hold values from -384 to 384
- lse: float32 [32, 16384], P('heads', 'seq'), may hold values from 0 to 20, as said below
Outputs:
- d_queries: bfloat16 [16384, 4096], P('seq', 'heads')
- key_gradient: bfloat16 [16384, 1024], P('seq', 'heads')
- value_gradient: bfloat16 [16384, 1024], P('seq', 'heads')
The draws below stay inside these ranges and needn't reach their ends.
Inputs may be any that keep to these rules, and one draw needn't show every extreme that they name: `lse`: positive and finite; one entry for each query head and position.
All inputs are finite; a program needn't handle non-finite values.
Results may differ from the reference program's by a relative error of at most 0.0054.
Values may be sent and summed in bfloat16 or wider, within the bound.
A program may use at most 128 MiB of HBM per device.

```python
import jax
import jax.numpy as jnp
from jax import lax

QUERY_HEADS = 32
KEY_VALUE_HEADS = 8
HEAD_SIZE = 128
WINDOW = 4096
TOK_DEV = 512
SEQUENCE_TOKENS = 16384


def draw_lse(key, part):
    positions = jnp.arange(SEQUENCE_TOKENS, dtype=jnp.int32)
    counted = jnp.minimum(positions + 1, WINDOW).astype(jnp.float32)
    offset = jax.random.uniform(jax.random.fold_in(key, 7), (QUERY_HEADS, SEQUENCE_TOKENS), jnp.float32, 0.0, 1.0)
    return jnp.log(counted)[None, :] + offset


def block_scale(rng, shape, cuts, low, top_value):
    def one(axis_at, shards_of):
        steps = jax.random.uniform(jax.random.fold_in(jax.random.fold_in(rng, 6), axis_at), (shards_of,), jnp.float32, low / len(cuts), top_value / len(cuts))
        return jnp.repeat(jnp.exp(steps), shape[axis_at] // shards_of).reshape((-1,) + (1,) * (len(shape) - axis_at - 1))

    factor_of = one(*cuts[0])
    for cut in cuts[1:]:
        factor_of = factor_of * one(*cut)
    return factor_of


def scatter_about(rng, dims, deviation, reach, cuts=(), kind=jnp.bfloat16):
    loudness = block_scale(rng, dims, cuts, -0.22, 0.18) if cuts else 1.0
    result = jax.random.normal(rng, dims, jnp.float32) * deviation * loudness
    return jnp.minimum(jnp.maximum(result, -reach), reach).astype(kind)


def setup_inputs(seed: int = 0) -> dict:
    seeds = jax.random.split(jax.random.key(seed), 7)
    return {
        "queries": scatter_about(seeds[0], (SEQUENCE_TOKENS, QUERY_HEADS * HEAD_SIZE), 1.0, 6.0, ((0, 32), (1, 4))),
        "keys": scatter_about(seeds[1], (SEQUENCE_TOKENS, KEY_VALUE_HEADS * HEAD_SIZE), 1.0, 6.0, ((0, 32), (1, 4))),
        "values": scatter_about(seeds[2], (SEQUENCE_TOKENS, KEY_VALUE_HEADS * HEAD_SIZE), 1.0, 6.0, ((0, 32), (1, 4))),
        "out": scatter_about(seeds[3], (SEQUENCE_TOKENS, QUERY_HEADS * HEAD_SIZE), 0.3, 1.796875, ((0, 32), (1, 4))),
        "output_gradient": scatter_about(seeds[4], (SEQUENCE_TOKENS, QUERY_HEADS * HEAD_SIZE), 64.0, 384.0, ((0, 32), (1, 4))),
        "lse": draw_lse(jax.random.fold_in(seeds[6], 71), 0),
    }


def reference(queries, keys, values, out, output_gradient, lse):
    count_tokens = queries.shape[0]
    group_ratio = QUERY_HEADS // KEY_VALUE_HEADS
    scale = HEAD_SIZE ** -0.5
    span = WINDOW + TOK_DEV
    blocks = count_tokens // TOK_DEV
    query_full = queries.reshape(count_tokens, KEY_VALUE_HEADS, group_ratio, HEAD_SIZE)
    output_gradient_full = output_gradient.reshape(count_tokens, KEY_VALUE_HEADS, group_ratio, HEAD_SIZE)
    key_full = keys.reshape(count_tokens, KEY_VALUE_HEADS, HEAD_SIZE)
    value_full = values.reshape(count_tokens, KEY_VALUE_HEADS, HEAD_SIZE)
    delta_rows = jnp.sum((output_gradient.astype(jnp.float32) * out.astype(jnp.float32)).reshape(count_tokens, QUERY_HEADS, HEAD_SIZE), axis=-1)
    delta_full = delta_rows.reshape(count_tokens, KEY_VALUE_HEADS, group_ratio)
    logsumexp_full = lse.T.reshape(count_tokens, KEY_VALUE_HEADS, group_ratio)

    def head_function(head):
        query_head = query_full[:, head]
        dout_head = output_gradient_full[:, head]
        delta_head = delta_full[:, head]
        lse_head = logsumexp_full[:, head]
        key_pad = jnp.concatenate([jnp.zeros((WINDOW, HEAD_SIZE), jnp.bfloat16), key_full[:, head]], axis=0)
        value_pad = jnp.concatenate([jnp.zeros((WINDOW, HEAD_SIZE), jnp.bfloat16), value_full[:, head]], axis=0)

        def visit(carry, block):
            dk_acc, dv_acc = carry
            qstart = (block * TOK_DEV).astype(jnp.int32)
            query_blk = lax.dynamic_slice_in_dim(query_head, qstart, TOK_DEV, 0).astype(jnp.float32)
            dout_blk = lax.dynamic_slice_in_dim(dout_head, qstart, TOK_DEV, 0).astype(jnp.float32)
            delta_blk = lax.dynamic_slice_in_dim(delta_head, qstart, TOK_DEV, 0)
            lse_blk = lax.dynamic_slice_in_dim(lse_head, qstart, TOK_DEV, 0)
            key_win = lax.dynamic_slice_in_dim(key_pad, qstart, span, 0).astype(jnp.float32)
            value_win = lax.dynamic_slice_in_dim(value_pad, qstart, span, 0).astype(jnp.float32)
            scores = jnp.einsum('qgd,sd->gqs', query_blk, key_win) * scale
            qpos = qstart + jnp.arange(TOK_DEV, dtype=jnp.int32)
            kpos = qstart - WINDOW + jnp.arange(span, dtype=jnp.int32)
            differ = qpos[:, None] - kpos[None, :]
            in_window = (differ >= 0) & (differ < WINDOW) & (kpos >= 0)[None, :]
            softmax_w = jnp.where(in_window[None], jnp.exp(scores - lse_blk.T[:, :, None]), jnp.float32(0.0))
            d_probs = jnp.einsum('qgd,sd->gqs', dout_blk, value_win)
            d_scores = (softmax_w * (d_probs - delta_blk.T[:, :, None]) * scale).astype(jnp.bfloat16).astype(jnp.float32)
            weights_b = softmax_w.astype(jnp.bfloat16).astype(jnp.float32)
            dv_part = jnp.einsum('gqs,qgd->sd', weights_b, dout_blk)
            dk_part = jnp.einsum('gqs,qgd->sd', d_scores, query_blk)
            dq_blk = jnp.einsum('gqs,sd->qgd', d_scores, key_win)
            dk_acc = lax.dynamic_update_slice_in_dim(dk_acc, lax.dynamic_slice_in_dim(dk_acc, qstart, span, 0) + dk_part, qstart, 0)
            dv_acc = lax.dynamic_update_slice_in_dim(dv_acc, lax.dynamic_slice_in_dim(dv_acc, qstart, span, 0) + dv_part, qstart, 0)
            return (dk_acc, dv_acc), dq_blk

        zeros_acc = jnp.zeros((WINDOW + count_tokens, HEAD_SIZE), jnp.float32)
        (dk_acc, dv_acc), dq_all = lax.scan(visit, (zeros_acc, zeros_acc), jnp.arange(blocks, dtype=jnp.int32))
        return dq_all.reshape(count_tokens, group_ratio, HEAD_SIZE), dk_acc[WINDOW:], dv_acc[WINDOW:]

    query_gradient_heads, key_gradient_heads, value_gradient_heads = lax.map(head_function, jnp.arange(KEY_VALUE_HEADS, dtype=jnp.int32))
    d_queries = jnp.transpose(query_gradient_heads, (1, 0, 2, 3)).reshape(count_tokens, QUERY_HEADS * HEAD_SIZE).astype(jnp.bfloat16)
    key_gradient = jnp.transpose(key_gradient_heads, (1, 0, 2)).reshape(count_tokens, KEY_VALUE_HEADS * HEAD_SIZE).astype(jnp.bfloat16)
    value_gradient = jnp.transpose(value_gradient_heads, (1, 0, 2)).reshape(count_tokens, KEY_VALUE_HEADS * HEAD_SIZE).astype(jnp.bfloat16)
    return (d_queries, key_gradient, value_gradient)
```

```python
import functools

import jax
import jax.numpy as jnp
from jax import lax
from jax.experimental import pallas as pl
from jax.experimental.pallas import tpu as pltpu
from jax.sharding import PartitionSpec as P

HEAD = 128
GROUP = 4
TOK = 512
SCALE = HEAD ** (-0.5)
LOG2E = 1.4426950408889634
f32, bf16 = jnp.float32, jnp.bfloat16
NT = (((1,), (1,)), ((), ()))
NN = (((1,), (0,)), ((), ()))
TN = (((0,), (0,)), ((), ()))

BACK = (0, 2, 4, 1, 3)
ITEMS = (
    (0, 0, 0), (0, 0, 1), (0, 1, 0), (0, 2, 0), (0, 1, 1), (0, 2, 1),
    (0, 3, 1), (0, 3, 0), (0, 4, 1), (0, 4, 0),
    (1, 3, 1), (1, 3, 0), (1, 4, 1), (1, 4, 0),
    (1, 1, 0), (1, 1, 1), (1, 2, 0), (1, 2, 1), (1, 0, 1), (1, 0, 0),
)


def dot(a, b, dims):
    return lax.dot_general(a, b, dims, preferred_element_type=f32)


def pick(i, values):
    out = jnp.int32(values[0])
    for j, v in enumerate(values):
        if j:
            out = jnp.where(i == j, jnp.int32(v), out)
    return out


def kernel(q_hbm, k_hbm, v_hbm, o_hbm, do_hbm, lse_ref, dq_hbm, dk_hbm, dv_hbm,
           qb, dob, doall, oall, ld, kvb, acc, dqt, stage, nb, ub, fin, mine, dqs,
           loc, out_sem, sp, rp, ss, rk, sm, rn, sd, ru, se, re):
    s = lax.axis_index("seq")
    hd = lax.axis_index("heads")
    row = s // 4
    x = lax.rem(s, 4)
    pi = x // 2
    m = lax.rem(x, 2)
    mo = 1 - m
    g = jnp.where(pi == 0, m, mo)
    go = 1 - g
    sup = 2 * row + pi
    rows = lax.axis_size("seq") // 4

    def at_row(k):
        return lax.rem(row + k + rows, rows) * 4 + x

    partner = row * 4 + pi * 2 + mo
    nbr = row * 4 + 3 - x
    up1, up2, down1, down2 = at_row(1), at_row(2), at_row(-1), at_row(-2)

    def rc(src, dst, send, recv, dest):
        return pltpu.make_async_remote_copy(
            src_ref=src, dst_ref=dst, send_sem=send, recv_sem=recv,
            device_id=(hd, dest), device_id_type=pl.DeviceIdType.MESH)

    def cols(n, width):
        return pl.ds(pl.multiple_of(n * width, width), width)

    local = [
        pltpu.make_async_copy(k_hbm.at[:, cols(g, HEAD)], kvb.at[0, m, 0], loc.at[0]),
        pltpu.make_async_copy(v_hbm.at[:, cols(g, HEAD)], kvb.at[0, m, 1], loc.at[1]),
        pltpu.make_async_copy(do_hbm, doall, loc.at[2]),
        pltpu.make_async_copy(o_hbm, oall, loc.at[3]),
        pltpu.make_async_copy(q_hbm.at[:, cols(g, 4 * HEAD)], qb.at[0], loc.at[4]),
        pltpu.make_async_copy(do_hbm.at[:, cols(g, 4 * HEAD)], dob.at[0], loc.at[5]),
    ]
    for c in local:
        c.start()

    barrier = pltpu.get_barrier_semaphore()
    for d in (partner, nbr, up1, up2, down1, down2):
        pl.semaphore_signal(barrier, inc=1, device_id=(hd, d), device_id_type=pl.DeviceIdType.MESH)
    pl.semaphore_wait(barrier, 6)

    pair = [
        rc(k_hbm.at[:, cols(go, HEAD)], kvb.at[0, m, 0], sp.at[0], rp.at[0], partner),
        rc(v_hbm.at[:, cols(go, HEAD)], kvb.at[0, m, 1], sp.at[1], rp.at[1], partner),
        rc(do_hbm.at[:, cols(go, 4 * HEAD)], dob.at[1], sp.at[2], rp.at[2], partner),
        rc(q_hbm.at[:, cols(go, 4 * HEAD)], qb.at[1], sp.at[3], rp.at[3], partner),
    ]
    for c in pair:
        c.start()
    ld_copy = rc(ld.at[0], ld.at[1], sp.at[4], rp.at[4], partner)

    def to_up1(h):
        return rc(kvb.at[0, h], kvb.at[1, h], ss.at[0, h], rk.at[1, h], up1)

    def to_up2(h):
        return rc(kvb.at[0, h], kvb.at[2, h], ss.at[1, h], rk.at[2, h], up2)

    def forward(src, dst, h):
        return rc(kvb.at[src, h], kvb.at[dst, h], ss.at[dst - 1, h], rk.at[dst, h], nbr)

    def arrived(slot, h):
        rc(kvb.at[slot, h], kvb.at[slot, h], ss.at[0, h], rk.at[slot, h], nbr).wait_recv()

    def own_out(h):
        to_up1(h).start()
        to_up2(h).start()

        @pl.when(pi == 0)
        def _():
            forward(0, 3, h).start()

    local[0].wait()
    local[1].wait()
    own_out(m)

    ld[0, 0:8, :] = lse_ref[...] * LOG2E
    local[2].wait()
    local[3].wait()
    for h in range(8):
        c = slice(h * HEAD, (h + 1) * HEAD)
        prod = doall[:, c].astype(f32) * oall[:, c].astype(f32)
        ld[0, 8 + h:9 + h, :] = jnp.sum(prod.T, axis=0, keepdims=True)
    ld_copy.start()
    acc[...] = jnp.zeros_like(acc)
    dqt[...] = jnp.zeros_like(dqt)
    local[4].wait()
    local[5].wait()

    def tile(qs, slot, kh, h, k0, q0, qn, mask):
        hs = cols(h, HEAD)
        q = qb[qs, q0:q0 + qn, hs]
        do = dob[qs, q0:q0 + qn, hs]
        lse = ld[qs, pl.ds(g * 4 + h, 1), q0:q0 + qn]
        delta = ld[qs, pl.ds(8 + g * 4 + h, 1), q0:q0 + qn]
        k = kvb[slot, kh, 0, k0:k0 + 256, :]
        v = kvb[slot, kh, 1, k0:k0 + 256, :]
        p = jnp.exp2(dot(k, q, NT) * (SCALE * LOG2E) - lse)
        if mask is not None:
            kk = lax.broadcasted_iota(jnp.int32, p.shape, 0) + k0
            qq = lax.broadcasted_iota(jnp.int32, p.shape, 1) + q0
            p = jnp.where(qq >= kk if mask == "low" else kk > qq, p, 0.0)
        ds = (p * (dot(v, do, NT) - delta)).astype(bf16)
        acc[slot, kh, 1, k0:k0 + 256, :] += dot(p.astype(bf16), do, NN)
        acc[slot, kh, 0, k0:k0 + 256, :] += dot(ds, q, NN)
        dqt[qs, h, :, q0:q0 + qn] += dot(k, ds, TN)

    shapes = {
        "full": ((0, 0, 512, None), (256, 0, 512, None)),
        "low": ((0, 0, 512, "low"), (256, 256, 256, "low")),
        "up": ((0, 0, 256, "up"), (256, 0, 512, "up")),
    }

    def work(qs, slot, kh, kind):
        @pl.loop(0, 2)
        def _(h2):
            for u in range(2):
                for k0, q0, qn, mask in shapes[kind]:
                    tile(qs, slot, kh, h2 * 2 + u, k0, q0, qn, mask)

    def send_partial(slot, h, copy):
        stage[slot, h] = acc[slot, h].astype(bf16)
        copy.start()

    def to_nbr(n, h):
        return rc(stage.at[3 + n, h], nb.at[n, h], sm.at[n, h], rn.at[n, h], nbr)

    def to_down(n, h):
        return rc(stage.at[1 + n, h], ub.at[n, h], sd.at[n, h], ru.at[n, h], down1 if n == 0 else down2)

    def add_nbr(slot, n, h):
        rc(nb.at[n, h], nb.at[n, h], sm.at[n, h], rn.at[n, h], nbr).wait_recv()
        acc[slot, h] = acc[slot, h] + nb[n, h].astype(f32)

    @pl.loop(0, len(ITEMS))
    def _(i):
        qs = pick(i, [a for a, _, _ in ITEMS])
        slot = pick(i, [b for _, b, _ in ITEMS])
        par = pick(i, [c for _, _, c in ITEMS])
        back = pick(i, [BACK[b] for _, b, _ in ITEMS])
        kh = jnp.where(par == 0, m, mo)
        mq = jnp.where(qs == 0, m, mo)

        @pl.when(i == 1)
        def _():
            pair_in = rc(kvb.at[0, mo, 0], kvb.at[0, mo, 0], sp.at[0], rp.at[0], partner)
            pair_in.wait_recv()
            rc(kvb.at[0, mo, 1], kvb.at[0, mo, 1], sp.at[1], rp.at[1], partner).wait_recv()
            own_out(mo)

        @pl.when((i >= 2) & (i < 10))
        def _():
            arrived(slot, kh)

            @pl.when(slot == 1)
            def _():
                forward(1, 4 - pi, kh).start()

            @pl.when((slot == 2) & (pi == 1))
            def _():
                forward(2, 4, kh).start()

        @pl.when(i == 10)
        def _():
            pair[2].wait_recv()
            pair[3].wait_recv()
            ld_copy.wait_recv()

        gap = 2 * back + mq - kh
        valid = sup >= back

        @pl.when(valid & (gap > 0) & (gap < 8))
        def _():
            work(qs, slot, kh, "full")

        @pl.when(valid & (gap == 0))
        def _():
            work(qs, slot, kh, "low")

        @pl.when(valid & (gap == 8))
        def _():
            work(qs, slot, kh, "up")

        @pl.when((i >= 10) & (i < 14))
        def _():
            send_partial(slot, kh, to_nbr(slot - 3, kh))

        @pl.when((i >= 14) & (i < 16))
        def _():
            add_nbr(1, 1 - pi, kh)
            send_partial(1, kh, to_down(0, kh))

        @pl.when((i >= 16) & (i < 18))
        def _():
            @pl.when(pi == 1)
            def _():
                add_nbr(2, 1, kh)

            send_partial(2, kh, to_down(1, kh))

    def dq_stage(qs):
        for h in range(GROUP):
            dqs[qs, :, h * HEAD:(h + 1) * HEAD] = (dqt[qs, h] * SCALE).T.astype(bf16)

    dq_stage(1)
    dq_out = rc(dqs.at[1], dq_hbm.at[:, cols(g, 4 * HEAD)], se.at[0], re.at[0], partner)
    dq_out.start()
    dq_stage(0)
    dq_own = pltpu.make_async_copy(dqs.at[0], dq_hbm.at[:, cols(g, 4 * HEAD)], out_sem.at[0])
    dq_own.start()

    def finish(h, dst):
        @pl.when(pi == 0)
        def _():
            add_nbr(0, 0, h)

        for n in range(2):
            rc(ub.at[n, h], ub.at[n, h], sd.at[n, h], ru.at[n, h], up1).wait_recv()
        total = acc[0, h] + ub[0, h].astype(f32) + ub[1, h].astype(f32)
        dst[0] = (total[0] * SCALE).astype(bf16)
        dst[1] = total[1].astype(bf16)

    finish(mo, fin)
    ends = [
        rc(fin.at[0], dk_hbm.at[:, cols(g, HEAD)], se.at[1], re.at[1], partner),
        rc(fin.at[1], dv_hbm.at[:, cols(g, HEAD)], se.at[2], re.at[2], partner),
    ]
    for c in ends:
        c.start()
    finish(m, mine)
    outs = [
        pltpu.make_async_copy(mine.at[0], dk_hbm.at[:, cols(g, HEAD)], out_sem.at[1]),
        pltpu.make_async_copy(mine.at[1], dv_hbm.at[:, cols(g, HEAD)], out_sem.at[2]),
    ]
    for c in outs:
        c.start()

    for c in pair:
        c.wait_send()
    ld_copy.wait_send()
    for h in range(2):
        to_up1(h).wait_send()
        to_up2(h).wait_send()
        forward(0, 3, h).wait_send()
        forward(0, 4, h).wait_send()
        for n in range(2):
            to_nbr(n, h).wait_send()
            to_down(n, h).wait_send()
    rc(dqs.at[1], dq_hbm.at[:, cols(go, 4 * HEAD)], se.at[0], re.at[0], partner).wait()
    rc(fin.at[0], dk_hbm.at[:, cols(go, HEAD)], se.at[1], re.at[1], partner).wait()
    rc(fin.at[1], dv_hbm.at[:, cols(go, HEAD)], se.at[2], re.at[2], partner).wait()
    dq_own.wait()
    for c in outs:
        c.wait()


def shards(queries, keys, values, out, output_gradient, lse):
    hbm = pl.BlockSpec(memory_space=pl.ANY)
    vm = pl.BlockSpec(memory_space=pltpu.VMEM)
    dma = pltpu.SemaphoreType.DMA
    return pl.pallas_call(
        kernel,
        out_shape=(
            jax.ShapeDtypeStruct(queries.shape, bf16),
            jax.ShapeDtypeStruct(keys.shape, bf16),
            jax.ShapeDtypeStruct(values.shape, bf16),
        ),
        in_specs=[hbm] * 5 + [vm],
        out_specs=(hbm, hbm, hbm),
        scratch_shapes=[
            pltpu.VMEM((2, TOK, 4 * HEAD), bf16),
            pltpu.VMEM((2, TOK, 4 * HEAD), bf16),
            pltpu.VMEM((TOK, 8 * HEAD), bf16),
            pltpu.VMEM((TOK, 8 * HEAD), bf16),
            pltpu.VMEM((2, 16, TOK), f32),
            pltpu.VMEM((5, 2, 2, TOK, HEAD), bf16),
            pltpu.VMEM((5, 2, 2, TOK, HEAD), f32),
            pltpu.VMEM((2, GROUP, HEAD, TOK), f32),
            pltpu.VMEM((5, 2, 2, TOK, HEAD), bf16),
            pltpu.VMEM((2, 2, 2, TOK, HEAD), bf16),
            pltpu.VMEM((2, 2, 2, TOK, HEAD), bf16),
            pltpu.VMEM((2, TOK, HEAD), bf16),
            pltpu.VMEM((2, TOK, HEAD), bf16),
            pltpu.VMEM((2, TOK, 4 * HEAD), bf16),
            dma((6,)), dma((3,)), dma((5,)), dma((5,)),
            dma((4, 2)), dma((5, 2)),
            dma((2, 2)), dma((2, 2)), dma((2, 2)), dma((2, 2)),
            dma((3,)), dma((3,)),
        ],
        compiler_params=pltpu.CompilerParams(
            collective_id=0, has_side_effects=True, vmem_limit_bytes=48 << 20),
        name="swa_bwd",
    )(queries, keys, values, out, output_gradient, lse)


def solution(mesh):
    return jax.shard_map(
        shards,
        mesh=mesh,
        in_specs=(P("seq", "heads"),) * 5 + (P("heads", "seq"),),
        out_specs=(P("seq", "heads"),) * 3,
        check_vma=False,
    )
```

```python
import functools

import jax
import jax.numpy as jnp
from jax import lax
from jax.experimental import pallas as pl
from jax.experimental.pallas import tpu as pltpu
from jax.sharding import PartitionSpec as P

HEAD = 128
GROUP = 4
TOK = 512
SCALE = HEAD ** (-0.5)
LOG2E = 1.4426950408889634
f32, bf16 = jnp.float32, jnp.bfloat16
NT = (((1,), (1,)), ((), ()))
NN = (((1,), (0,)), ((), ()))
TN = (((0,), (0,)), ((), ()))

BACK = (0, 2, 4, 1, 3)
ITEMS = (
    (
        (0, 0, 0), (0, 0, 1), (0, 1, 0), (0, 2, 0), (0, 1, 1),
        (0, 3, 1), (0, 2, 1), (0, 3, 0), (0, 4, 1), (0, 4, 0),
        (1, 3, 0), (1, 3, 1), (1, 4, 0), (1, 4, 1), (1, 2, 1),
        (1, 2, 0), (1, 1, 1), (1, 1, 0), (1, 0, 1), (1, 0, 0),
    ),
    (
        (0, 0, 0), (0, 0, 1), (0, 3, 1), (0, 1, 0), (0, 2, 0),
        (0, 3, 0), (0, 1, 1), (0, 2, 1), (0, 4, 1), (0, 4, 0),
        (1, 4, 0), (1, 4, 1), (1, 3, 0), (1, 3, 1), (1, 1, 1),
        (1, 1, 0), (1, 2, 1), (1, 2, 0), (1, 0, 1), (1, 0, 0),
    ),
)


def dot(a, b, dims):
    return lax.dot_general(a, b, dims, preferred_element_type=f32)


def pick(i, values):
    out = jnp.int32(values[0])
    for j, v in enumerate(values):
        if j:
            out = jnp.where(i == j, jnp.int32(v), out)
    return out


def kernel(q_hbm, k_hbm, v_hbm, o_hbm, do_hbm, lse_ref, dq_hbm, dk_hbm, dv_hbm,
           qb, dob, doall, oall, ld, kvb, acc, dqt, stage, nb, ub, fin, mine, dqs,
           loc, out_sem, sp, rp, ss, rk, sm, rn, sd, ru, se, re):
    s = lax.axis_index("seq")
    hd = lax.axis_index("heads")
    row = s // 4
    x = lax.rem(s, 4)
    pi = x // 2
    m = lax.rem(x, 2)
    mo = 1 - m
    g = jnp.where(pi == 0, m, mo)
    go = 1 - g
    sup = 2 * row + pi
    rows = lax.axis_size("seq") // 4

    def at_row(k):
        return lax.rem(row + k + rows, rows) * 4 + x

    partner = row * 4 + pi * 2 + mo
    nbr = row * 4 + 3 - x
    up1, up2, down1, down2 = at_row(1), at_row(2), at_row(-1), at_row(-2)

    def rc(src, dst, send, recv, dest):
        return pltpu.make_async_remote_copy(
            src_ref=src, dst_ref=dst, send_sem=send, recv_sem=recv,
            device_id=(hd, dest), device_id_type=pl.DeviceIdType.MESH)

    def cols(n, width):
        return pl.ds(pl.multiple_of(n * width, width), width)

    local = [
        pltpu.make_async_copy(k_hbm.at[:, cols(g, HEAD)], kvb.at[0, m, 0], loc.at[0]),
        pltpu.make_async_copy(v_hbm.at[:, cols(g, HEAD)], kvb.at[0, m, 1], loc.at[1]),
        pltpu.make_async_copy(do_hbm, doall, loc.at[2]),
        pltpu.make_async_copy(o_hbm, oall, loc.at[3]),
        pltpu.make_async_copy(q_hbm.at[:, cols(g, 4 * HEAD)], qb.at[0], loc.at[4]),
        pltpu.make_async_copy(do_hbm.at[:, cols(g, 4 * HEAD)], dob.at[0], loc.at[5]),
    ]
    for c in local:
        c.start()

    barrier = pltpu.get_barrier_semaphore()
    for d in (partner, nbr, up1, up2, down1, down2):
        pl.semaphore_signal(barrier, inc=1, device_id=(hd, d), device_id_type=pl.DeviceIdType.MESH)
    pl.semaphore_wait(barrier, 6)

    pair = [
        rc(k_hbm.at[:, cols(go, HEAD)], kvb.at[0, m, 0], sp.at[0], rp.at[0], partner),
        rc(v_hbm.at[:, cols(go, HEAD)], kvb.at[0, m, 1], sp.at[1], rp.at[1], partner),
        rc(do_hbm.at[:, cols(go, 4 * HEAD)], dob.at[1], sp.at[2], rp.at[2], partner),
        rc(q_hbm.at[:, cols(go, 4 * HEAD)], qb.at[1], sp.at[3], rp.at[3], partner),
    ]
    for c in pair:
        c.start()
    ld_copy = rc(ld.at[0], ld.at[1], sp.at[4], rp.at[4], partner)

    def to_up1(h):
        return rc(kvb.at[0, h], kvb.at[1, h], ss.at[0, h], rk.at[1, h], up1)

    def to_up2(h):
        return rc(kvb.at[0, h], kvb.at[2, h], ss.at[1, h], rk.at[2, h], up2)

    def forward(src, dst, h):
        return rc(kvb.at[src, h], kvb.at[dst, h], ss.at[dst - 1, h], rk.at[dst, h], nbr)

    def arrived(slot, h):
        rc(kvb.at[slot, h], kvb.at[slot, h], ss.at[0, h], rk.at[slot, h], nbr).wait_recv()

    def own_out(h):
        to_up1(h).start()
        to_up2(h).start()

        @pl.when(pi == 0)
        def _():
            forward(0, 3, h).start()

    local[0].wait()
    local[1].wait()
    own_out(m)

    ld[0, 0:8, :] = lse_ref[...] * LOG2E
    local[2].wait()
    local[3].wait()
    for h in range(8):
        c = slice(h * HEAD, (h + 1) * HEAD)
        prod = doall[:, c].astype(f32) * oall[:, c].astype(f32)
        ld[0, 8 + h:9 + h, :] = jnp.sum(prod.T, axis=0, keepdims=True)
    ld_copy.start()
    acc[...] = jnp.zeros_like(acc)
    dqt[...] = jnp.zeros_like(dqt)
    local[4].wait()
    local[5].wait()

    def tile(qs, slot, kh, h, k0, q0, qn, mask):
        hs = cols(h, HEAD)
        q = qb[qs, q0:q0 + qn, hs]
        do = dob[qs, q0:q0 + qn, hs]
        lse = ld[qs, pl.ds(g * 4 + h, 1), q0:q0 + qn]
        delta = ld[qs, pl.ds(8 + g * 4 + h, 1), q0:q0 + qn]
        k = kvb[slot, kh, 0, k0:k0 + 256, :]
        v = kvb[slot, kh, 1, k0:k0 + 256, :]
        p = jnp.exp2(dot(k, q, NT) * (SCALE * LOG2E) - lse)
        if mask is not None:
            kk = lax.broadcasted_iota(jnp.int32, p.shape, 0) + k0
            qq = lax.broadcasted_iota(jnp.int32, p.shape, 1) + q0
            p = jnp.where(qq >= kk if mask == "low" else kk > qq, p, 0.0)
        ds = (p * (dot(v, do, NT) - delta)).astype(bf16)
        acc[slot, kh, 1, k0:k0 + 256, :] += dot(p.astype(bf16), do, NN)
        acc[slot, kh, 0, k0:k0 + 256, :] += dot(ds, q, NN)
        dqt[qs, h, :, q0:q0 + qn] += dot(k, ds, TN)

    shapes = {
        "full": ((0, 0, 512, None), (256, 0, 512, None)),
        "low": ((0, 0, 512, "low"), (256, 256, 256, "low")),
        "up": ((0, 0, 256, "up"), (256, 0, 512, "up")),
    }

    def work(qs, slot, kh, kind):
        @pl.loop(0, 2)
        def _(h2):
            for u in range(2):
                for k0, q0, qn, mask in shapes[kind]:
                    tile(qs, slot, kh, h2 * 2 + u, k0, q0, qn, mask)

    def send_partial(slot, h, copy):
        stage[slot, h] = acc[slot, h].astype(bf16)
        copy.start()

    def to_nbr(n, h):
        return rc(stage.at[3 + n, h], nb.at[n, h], sm.at[n, h], rn.at[n, h], nbr)

    def to_down(n, h):
        return rc(stage.at[1 + n, h], ub.at[n, h], sd.at[n, h], ru.at[n, h], down1 if n == 0 else down2)

    def add_nbr(slot, n, h):
        rc(nb.at[n, h], nb.at[n, h], sm.at[n, h], rn.at[n, h], nbr).wait_recv()
        acc[slot, h] = acc[slot, h] + nb[n, h].astype(f32)

    @pl.loop(0, 20)
    def _(i):
        at = i + 20 * pi
        items = ITEMS[0] + ITEMS[1]
        qs = pick(at, [a for a, _, _ in items])
        slot = pick(at, [b for _, b, _ in items])
        par = pick(at, [c for _, _, c in items])
        back = pick(slot, BACK)
        kh = jnp.where(par == 0, m, mo)
        mq = jnp.where(qs == 0, m, mo)

        @pl.when(i == 1)
        def _():
            pair_in = rc(kvb.at[0, mo, 0], kvb.at[0, mo, 0], sp.at[0], rp.at[0], partner)
            pair_in.wait_recv()
            rc(kvb.at[0, mo, 1], kvb.at[0, mo, 1], sp.at[1], rp.at[1], partner).wait_recv()
            own_out(mo)

        @pl.when((i >= 2) & (i < 10))
        def _():
            arrived(slot, kh)

            @pl.when(slot == 1)
            def _():
                forward(1, 4 - pi, kh).start()

            @pl.when((slot == 2) & (pi == 1))
            def _():
                forward(2, 4, kh).start()

        @pl.when(i == 10)
        def _():
            pair[2].wait_recv()
            pair[3].wait_recv()
            ld_copy.wait_recv()

        gap = 2 * back + mq - kh
        valid = sup >= back

        @pl.when(valid & (gap > 0) & (gap < 8))
        def _():
            work(qs, slot, kh, "full")

        @pl.when(valid & (gap == 0))
        def _():
            work(qs, slot, kh, "low")

        @pl.when(valid & (gap == 8))
        def _():
            work(qs, slot, kh, "up")

        @pl.when((qs == 1) & (slot >= 3))
        def _():
            send_partial(slot, kh, to_nbr(slot - 3, kh))

        @pl.when((qs == 1) & (slot == 1))
        def _():
            add_nbr(1, 1 - pi, kh)
            send_partial(1, kh, to_down(0, kh))

        @pl.when((qs == 1) & (slot == 2) & (pi == 0))
        def _():
            send_partial(2, kh, to_down(1, kh))

    def dq_stage(qs):
        for h in range(GROUP):
            dqs[qs, :, h * HEAD:(h + 1) * HEAD] = (dqt[qs, h] * SCALE).T.astype(bf16)

    dq_stage(1)
    dq_out = rc(dqs.at[1], dq_hbm.at[:, cols(g, 4 * HEAD)], se.at[0], re.at[0], partner)
    dq_out.start()

    @pl.when(pi == 1)
    def _():
        for h in (mo, m):
            add_nbr(2, 1, h)
            send_partial(2, h, to_down(1, h))

    dq_stage(0)
    dq_own = pltpu.make_async_copy(dqs.at[0], dq_hbm.at[:, cols(g, 4 * HEAD)], out_sem.at[0])
    dq_own.start()

    def finish(h, dst):
        @pl.when(pi == 0)
        def _():
            add_nbr(0, 0, h)

        for n in range(2):
            rc(ub.at[n, h], ub.at[n, h], sd.at[n, h], ru.at[n, h], up1).wait_recv()
        total = acc[0, h] + ub[0, h].astype(f32) + ub[1, h].astype(f32)
        dst[0] = (total[0] * SCALE).astype(bf16)
        dst[1] = total[1].astype(bf16)

    finish(mo, fin)
    ends = [
        rc(fin.at[0], dk_hbm.at[:, cols(g, HEAD)], se.at[1], re.at[1], partner),
        rc(fin.at[1], dv_hbm.at[:, cols(g, HEAD)], se.at[2], re.at[2], partner),
    ]
    for c in ends:
        c.start()
    finish(m, mine)
    outs = [
        pltpu.make_async_copy(mine.at[0], dk_hbm.at[:, cols(g, HEAD)], out_sem.at[1]),
        pltpu.make_async_copy(mine.at[1], dv_hbm.at[:, cols(g, HEAD)], out_sem.at[2]),
    ]
    for c in outs:
        c.start()

    for c in pair:
        c.wait_send()
    ld_copy.wait_send()
    for h in range(2):
        to_up1(h).wait_send()
        to_up2(h).wait_send()
        forward(0, 3, h).wait_send()
        forward(0, 4, h).wait_send()
        for n in range(2):
            to_nbr(n, h).wait_send()
            to_down(n, h).wait_send()
    rc(dqs.at[1], dq_hbm.at[:, cols(go, 4 * HEAD)], se.at[0], re.at[0], partner).wait()
    rc(fin.at[0], dk_hbm.at[:, cols(go, HEAD)], se.at[1], re.at[1], partner).wait()
    rc(fin.at[1], dv_hbm.at[:, cols(go, HEAD)], se.at[2], re.at[2], partner).wait()
    dq_own.wait()
    for c in outs:
        c.wait()


def shards(queries, keys, values, out, output_gradient, lse):
    hbm = pl.BlockSpec(memory_space=pl.ANY)
    vm = pl.BlockSpec(memory_space=pltpu.VMEM)
    dma = pltpu.SemaphoreType.DMA
    return pl.pallas_call(
        kernel,
        out_shape=(
            jax.ShapeDtypeStruct(queries.shape, bf16),
            jax.ShapeDtypeStruct(keys.shape, bf16),
            jax.ShapeDtypeStruct(values.shape, bf16),
        ),
        in_specs=[hbm] * 5 + [vm],
        out_specs=(hbm, hbm, hbm),
        scratch_shapes=[
            pltpu.VMEM((2, TOK, 4 * HEAD), bf16),
            pltpu.VMEM((2, TOK, 4 * HEAD), bf16),
            pltpu.VMEM((TOK, 8 * HEAD), bf16),
            pltpu.VMEM((TOK, 8 * HEAD), bf16),
            pltpu.VMEM((2, 16, TOK), f32),
            pltpu.VMEM((5, 2, 2, TOK, HEAD), bf16),
            pltpu.VMEM((5, 2, 2, TOK, HEAD), f32),
            pltpu.VMEM((2, GROUP, HEAD, TOK), f32),
            pltpu.VMEM((5, 2, 2, TOK, HEAD), bf16),
            pltpu.VMEM((2, 2, 2, TOK, HEAD), bf16),
            pltpu.VMEM((2, 2, 2, TOK, HEAD), bf16),
            pltpu.VMEM((2, TOK, HEAD), bf16),
            pltpu.VMEM((2, TOK, HEAD), bf16),
            pltpu.VMEM((2, TOK, 4 * HEAD), bf16),
            dma((6,)), dma((3,)), dma((5,)), dma((5,)),
            dma((4, 2)), dma((5, 2)),
            dma((2, 2)), dma((2, 2)), dma((2, 2)), dma((2, 2)),
            dma((3,)), dma((3,)),
        ],
        compiler_params=pltpu.CompilerParams(
            collective_id=0, has_side_effects=True, vmem_limit_bytes=48 << 20),
        name="swa_bwd",
    )(queries, keys, values, out, output_gradient, lse)


def solution(mesh):
    return jax.shard_map(
        shards,
        mesh=mesh,
        in_specs=(P("seq", "heads"),) * 5 + (P("heads", "seq"),),
        out_specs=(P("seq", "heads"),) * 3,
        check_vma=False,
    )
```

```python
import functools

import jax
import jax.numpy as jnp
from jax import lax
from jax.experimental import pallas as pl
from jax.experimental.pallas import tpu as pltpu
from jax.sharding import PartitionSpec as P

HEAD = 128
GROUP = 4
TOK = 512
SCALE = HEAD ** (-0.5)
LOG2E = 1.4426950408889634
f32, bf16 = jnp.float32, jnp.bfloat16
NT = (((1,), (1,)), ((), ()))
NN = (((1,), (0,)), ((), ()))
TN = (((0,), (0,)), ((), ()))

BACK = (0, 2, 4, 1, 3)
ITEMS = (
    (
        (0, 0, 0), (0, 0, 1), (0, 2, 0), (0, 1, 0), (0, 2, 1),
        (0, 1, 1), (0, 3, 1), (0, 3, 0), (0, 4, 1), (0, 4, 0),
        (1, 3, 0), (1, 3, 1), (1, 4, 0), (1, 4, 1), (1, 2, 1),
        (1, 2, 0), (1, 1, 1), (1, 1, 0), (1, 0, 1), (1, 0, 0),
    ),
    (
        (0, 0, 0), (0, 0, 1), (0, 3, 1), (0, 2, 0), (0, 1, 0),
        (0, 2, 1), (0, 1, 1), (0, 3, 0), (0, 4, 1), (0, 4, 0),
        (1, 4, 0), (1, 4, 1), (1, 3, 0), (1, 3, 1), (1, 1, 1),
        (1, 1, 0), (1, 2, 1), (1, 2, 0), (1, 0, 1), (1, 0, 0),
    ),
)


def dot(a, b, dims):
    return lax.dot_general(a, b, dims, preferred_element_type=f32)


def pick(i, values):
    out = jnp.int32(values[0])
    for j, v in enumerate(values):
        if j:
            out = jnp.where(i == j, jnp.int32(v), out)
    return out


def kernel(q_hbm, k_hbm, v_hbm, o_hbm, do_hbm, lse_ref, dq_hbm, dk_hbm, dv_hbm,
           qb, dob, doall, oall, ld, kvb, acc, dqt, stage, nb, ub, fin, mine, dqs,
           loc, out_sem, sp, rp, ss, rk, sm, rn, sd, ru, se, re):
    s = lax.axis_index("seq")
    hd = lax.axis_index("heads")
    row = s // 4
    x = lax.rem(s, 4)
    pi = x // 2
    m = lax.rem(x, 2)
    mo = 1 - m
    g = jnp.where(pi == 0, m, mo)
    go = 1 - g
    sup = 2 * row + pi
    rows = lax.axis_size("seq") // 4

    def at_row(k):
        return lax.rem(row + k + rows, rows) * 4 + x

    partner = row * 4 + pi * 2 + mo
    nbr = row * 4 + 3 - x
    up1, up2, down1, down2 = at_row(1), at_row(2), at_row(-1), at_row(-2)

    def rc(src, dst, send, recv, dest):
        return pltpu.make_async_remote_copy(
            src_ref=src, dst_ref=dst, send_sem=send, recv_sem=recv,
            device_id=(hd, dest), device_id_type=pl.DeviceIdType.MESH)

    def cols(n, width):
        return pl.ds(pl.multiple_of(n * width, width), width)

    local = [
        pltpu.make_async_copy(k_hbm.at[:, cols(g, HEAD)], kvb.at[0, m, 0], loc.at[0]),
        pltpu.make_async_copy(v_hbm.at[:, cols(g, HEAD)], kvb.at[0, m, 1], loc.at[1]),
        pltpu.make_async_copy(do_hbm, doall, loc.at[2]),
        pltpu.make_async_copy(o_hbm, oall, loc.at[3]),
        pltpu.make_async_copy(q_hbm.at[:, cols(g, 4 * HEAD)], qb.at[0], loc.at[4]),
        pltpu.make_async_copy(do_hbm.at[:, cols(g, 4 * HEAD)], dob.at[0], loc.at[5]),
    ]
    for c in local:
        c.start()

    barrier = pltpu.get_barrier_semaphore()
    for d in (partner, nbr, up1, up2, down1, down2):
        pl.semaphore_signal(barrier, inc=1, device_id=(hd, d), device_id_type=pl.DeviceIdType.MESH)
    pl.semaphore_wait(barrier, 6)

    pair = [
        rc(k_hbm.at[:, cols(go, HEAD)], kvb.at[0, m, 0], sp.at[0], rp.at[0], partner),
        rc(v_hbm.at[:, cols(go, HEAD)], kvb.at[0, m, 1], sp.at[1], rp.at[1], partner),
        rc(do_hbm.at[:, cols(go, 4 * HEAD)], dob.at[1], sp.at[2], rp.at[2], partner),
        rc(q_hbm.at[:, cols(go, 4 * HEAD)], qb.at[1], sp.at[3], rp.at[3], partner),
    ]
    for c in pair:
        c.start()
    ld_copy = rc(ld.at[0], ld.at[1], sp.at[4], rp.at[4], partner)

    def to_up1(h):
        return rc(kvb.at[0, h], kvb.at[1, h], ss.at[0, h], rk.at[1, h], up1)

    def to_up2(h):
        return rc(kvb.at[0, h], kvb.at[2, h], ss.at[1, h], rk.at[2, h], up2)

    def forward(src, dst, h):
        return rc(kvb.at[src, h], kvb.at[dst, h], ss.at[dst - 1, h], rk.at[dst, h], nbr)

    def arrived(slot, h):
        rc(kvb.at[slot, h], kvb.at[slot, h], ss.at[0, h], rk.at[slot, h], nbr).wait_recv()

    def relay(h):
        return rc(kvb.at[2, h], kvb.at[1, h], ss.at[0, h], rk.at[1, h], down1)

    def own_out(h):
        to_up2(h).start()

        @pl.when(lax.rem(row, 2) == 0)
        def _():
            to_up1(h).start()

        @pl.when(pi == 0)
        def _():
            forward(0, 3, h).start()

    local[0].wait()
    local[1].wait()
    own_out(m)

    ld[0, 0:8, :] = lse_ref[...] * LOG2E
    local[2].wait()
    local[3].wait()
    for h in range(8):
        c = slice(h * HEAD, (h + 1) * HEAD)
        prod = doall[:, c].astype(f32) * oall[:, c].astype(f32)
        ld[0, 8 + h:9 + h, :] = jnp.sum(prod.T, axis=0, keepdims=True)
    ld_copy.start()
    acc[...] = jnp.zeros_like(acc)
    dqt[...] = jnp.zeros_like(dqt)
    local[4].wait()
    local[5].wait()

    def tile(qs, slot, kh, h, k0, q0, qn, mask):
        hs = cols(h, HEAD)
        q = qb[qs, q0:q0 + qn, hs]
        do = dob[qs, q0:q0 + qn, hs]
        lse = ld[qs, pl.ds(g * 4 + h, 1), q0:q0 + qn]
        delta = ld[qs, pl.ds(8 + g * 4 + h, 1), q0:q0 + qn]
        k = kvb[slot, kh, 0, k0:k0 + 256, :]
        v = kvb[slot, kh, 1, k0:k0 + 256, :]
        p = jnp.exp2(dot(k, q, NT) * (SCALE * LOG2E) - lse)
        if mask is not None:
            kk = lax.broadcasted_iota(jnp.int32, p.shape, 0) + k0
            qq = lax.broadcasted_iota(jnp.int32, p.shape, 1) + q0
            p = jnp.where(qq >= kk if mask == "low" else kk > qq, p, 0.0)
        ds = (p * (dot(v, do, NT) - delta)).astype(bf16)
        acc[slot, kh, 1, k0:k0 + 256, :] += dot(p.astype(bf16), do, NN)
        acc[slot, kh, 0, k0:k0 + 256, :] += dot(ds, q, NN)
        dqt[qs, h, :, q0:q0 + qn] += dot(k, ds, TN)

    shapes = {
        "full": ((0, 0, 512, None), (256, 0, 512, None)),
        "low": ((0, 0, 512, "low"), (256, 256, 256, "low")),
        "up": ((0, 0, 256, "up"), (256, 0, 512, "up")),
    }

    def work(qs, slot, kh, kind):
        @pl.loop(0, 2)
        def _(h2):
            for u in range(2):
                for k0, q0, qn, mask in shapes[kind]:
                    tile(qs, slot, kh, h2 * 2 + u, k0, q0, qn, mask)

    def send_partial(slot, h, copy):
        stage[slot, h] = acc[slot, h].astype(bf16)
        copy.start()

    def to_nbr(n, h):
        return rc(stage.at[3 + n, h], nb.at[n, h], sm.at[n, h], rn.at[n, h], nbr)

    def to_down(n, h):
        return rc(stage.at[1 + n, h], ub.at[n, h], sd.at[n, h], ru.at[n, h], down1 if n == 0 else down2)

    def add_nbr(slot, n, h):
        rc(nb.at[n, h], nb.at[n, h], sm.at[n, h], rn.at[n, h], nbr).wait_recv()
        acc[slot, h] = acc[slot, h] + nb[n, h].astype(f32)

    @pl.loop(0, 20)
    def _(i):
        at = i + 20 * pi
        items = ITEMS[0] + ITEMS[1]
        qs = pick(at, [a for a, _, _ in items])
        slot = pick(at, [b for _, b, _ in items])
        par = pick(at, [c for _, _, c in items])
        back = pick(slot, BACK)
        kh = jnp.where(par == 0, m, mo)
        mq = jnp.where(qs == 0, m, mo)

        @pl.when(i == 0)
        def _():
            pair_in = rc(kvb.at[0, mo, 0], kvb.at[0, mo, 0], sp.at[0], rp.at[0], partner)
            pair_in.wait_recv()
            rc(kvb.at[0, mo, 1], kvb.at[0, mo, 1], sp.at[1], rp.at[1], partner).wait_recv()
            own_out(mo)

        @pl.when((i >= 2) & (i < 10))
        def _():
            arrived(slot, kh)

            @pl.when((slot == 2) & (lax.rem(row, 2) == 1))
            def _():
                relay(kh).start()

            @pl.when(slot == 1)
            def _():
                forward(1, 4 - pi, kh).start()

            @pl.when((slot == 2) & (pi == 1))
            def _():
                forward(2, 4, kh).start()

        @pl.when(i == 10)
        def _():
            pair[2].wait_recv()
            pair[3].wait_recv()
            ld_copy.wait_recv()

        gap = 2 * back + mq - kh
        valid = sup >= back

        @pl.when(valid & (gap > 0) & (gap < 8))
        def _():
            work(qs, slot, kh, "full")

        @pl.when(valid & (gap == 0))
        def _():
            work(qs, slot, kh, "low")

        @pl.when(valid & (gap == 8))
        def _():
            work(qs, slot, kh, "up")

        @pl.when((qs == 1) & (slot >= 3))
        def _():
            send_partial(slot, kh, to_nbr(slot - 3, kh))

        @pl.when((qs == 1) & (slot == 1))
        def _():
            add_nbr(1, 1 - pi, kh)
            send_partial(1, kh, to_down(0, kh))

        @pl.when((qs == 1) & (slot == 2) & (pi == 0))
        def _():
            send_partial(2, kh, to_down(1, kh))

    def dq_stage(qs):
        for h in range(GROUP):
            dqs[qs, :, h * HEAD:(h + 1) * HEAD] = (dqt[qs, h] * SCALE).T.astype(bf16)

    dq_stage(1)
    dq_out = rc(dqs.at[1], dq_hbm.at[:, cols(g, 4 * HEAD)], se.at[0], re.at[0], partner)
    dq_out.start()

    @pl.when(pi == 1)
    def _():
        for h in (mo, m):
            add_nbr(2, 1, h)
            send_partial(2, h, to_down(1, h))

    dq_stage(0)
    dq_own = pltpu.make_async_copy(dqs.at[0], dq_hbm.at[:, cols(g, 4 * HEAD)], out_sem.at[0])
    dq_own.start()

    def finish(h, dst):
        @pl.when(pi == 0)
        def _():
            add_nbr(0, 0, h)

        for n in range(2):
            rc(ub.at[n, h], ub.at[n, h], sd.at[n, h], ru.at[n, h], up1).wait_recv()
        total = acc[0, h] + ub[0, h].astype(f32) + ub[1, h].astype(f32)
        dst[0] = (total[0] * SCALE).astype(bf16)
        dst[1] = total[1].astype(bf16)

    finish(mo, fin)
    ends = [
        rc(fin.at[0], dk_hbm.at[:, cols(g, HEAD)], se.at[1], re.at[1], partner),
        rc(fin.at[1], dv_hbm.at[:, cols(g, HEAD)], se.at[2], re.at[2], partner),
    ]
    for c in ends:
        c.start()
    finish(m, mine)
    outs = [
        pltpu.make_async_copy(mine.at[0], dk_hbm.at[:, cols(g, HEAD)], out_sem.at[1]),
        pltpu.make_async_copy(mine.at[1], dv_hbm.at[:, cols(g, HEAD)], out_sem.at[2]),
    ]
    for c in outs:
        c.start()

    for c in pair:
        c.wait_send()
    ld_copy.wait_send()
    for h in range(2):
        to_up1(h).wait_send()
        to_up2(h).wait_send()
        forward(0, 3, h).wait_send()
        forward(0, 4, h).wait_send()
        for n in range(2):
            to_nbr(n, h).wait_send()
            to_down(n, h).wait_send()
    rc(dqs.at[1], dq_hbm.at[:, cols(go, 4 * HEAD)], se.at[0], re.at[0], partner).wait()
    rc(fin.at[0], dk_hbm.at[:, cols(go, HEAD)], se.at[1], re.at[1], partner).wait()
    rc(fin.at[1], dv_hbm.at[:, cols(go, HEAD)], se.at[2], re.at[2], partner).wait()
    dq_own.wait()
    for c in outs:
        c.wait()


def shards(queries, keys, values, out, output_gradient, lse):
    hbm = pl.BlockSpec(memory_space=pl.ANY)
    vm = pl.BlockSpec(memory_space=pltpu.VMEM)
    dma = pltpu.SemaphoreType.DMA
    return pl.pallas_call(
        kernel,
        out_shape=(
            jax.ShapeDtypeStruct(queries.shape, bf16),
            jax.ShapeDtypeStruct(keys.shape, bf16),
            jax.ShapeDtypeStruct(values.shape, bf16),
        ),
        in_specs=[hbm] * 5 + [vm],
        out_specs=(hbm, hbm, hbm),
        scratch_shapes=[
            pltpu.VMEM((2, TOK, 4 * HEAD), bf16),
            pltpu.VMEM((2, TOK, 4 * HEAD), bf16),
            pltpu.VMEM((TOK, 8 * HEAD), bf16),
            pltpu.VMEM((TOK, 8 * HEAD), bf16),
            pltpu.VMEM((2, 16, TOK), f32),
            pltpu.VMEM((5, 2, 2, TOK, HEAD), bf16),
            pltpu.VMEM((5, 2, 2, TOK, HEAD), f32),
            pltpu.VMEM((2, GROUP, HEAD, TOK), f32),
            pltpu.VMEM((5, 2, 2, TOK, HEAD), bf16),
            pltpu.VMEM((2, 2, 2, TOK, HEAD), bf16),
            pltpu.VMEM((2, 2, 2, TOK, HEAD), bf16),
            pltpu.VMEM((2, TOK, HEAD), bf16),
            pltpu.VMEM((2, TOK, HEAD), bf16),
            pltpu.VMEM((2, TOK, 4 * HEAD), bf16),
            dma((6,)), dma((3,)), dma((5,)), dma((5,)),
            dma((4, 2)), dma((5, 2)),
            dma((2, 2)), dma((2, 2)), dma((2, 2)), dma((2, 2)),
            dma((3,)), dma((3,)),
        ],
        compiler_params=pltpu.CompilerParams(
            collective_id=0, has_side_effects=True, vmem_limit_bytes=48 << 20),
        name="swa_bwd",
    )(queries, keys, values, out, output_gradient, lse)


def solution(mesh):
    return jax.shard_map(
        shards,
        mesh=mesh,
        in_specs=(P("seq", "heads"),) * 5 + (P("heads", "seq"),),
        out_specs=(P("seq", "heads"),) * 3,
        check_vma=False,
    )
```
